256 devices in a mesh: grp: 8 (over x, core), rep: 32 (over z, y).
Axes of the slice: x: 4, y: 4, z: 8, core: 2. Of those that a mesh axis runs over, the one named last changes fastest.
Arguments:
- tokens: bfloat16 [131072, 1024], P(('grp', 'rep')), may hold values from -42 to 42
- owner: int32 [131072, 1], P(('grp', 'rep')), may hold values from 0 to 7; in each aligned block of 512 rows (0 to 511, 512 to 1023, ...) at most 128 rows name the same one
- list_local: int32 [131072], P(('grp', 'rep')), may hold values from 0 to 1023
- centroids: bfloat16 [262144, 1024], P(('grp', 'rep')), may hold values from -5 to 5
- rotation: bfloat16 [1024, 1024], replicated, may hold values from -0.1875 to 0.1875
- codebook: float32 [16, 64, 256], replicated, may hold values from -7 to 7
Outputs:
- new_codebook: float32 [16, 64, 256], replicated
- cross_cov: float32 [1024, 1024], P(('grp', 'rep'))
The draws below stay inside these ranges and needn't reach their ends.
Inputs may be any that keep to these rules, and one draw needn't show every extreme that they name: Among the rows of one device at most 128 name the same owner, and some device has exactly 128 for some owner.
All inputs are finite; a program needn't handle non-finite values.
Results may differ from the reference program's by a relative error of at most 0.0048.
The reference program's roundings to bfloat16 on the way (of `residual` and `rebuilt`) count: a program that leaves them out, or rounds other values in their place, can miss the bound.
Values may be sent and summed in bfloat16 or wider, within the bound.
No kernel may reach another device: no remote copies, remote signals or barrier semaphores. Data moves between devices by JAX's collectives and lax.ppermute only.
A program may use at most 64 MiB of HBM per device.

```python
import math
import jax
import jax.numpy as jnp
import numpy as np
from jax import lax

D = 1024
M = 16
K = 256
DSUB = 64
ROW_DEV = 512
LIST_DEV = 1024
OWNERS = 8
REPS = 32
CAP = 128
ROWS = 131072
NLIST = 262144


def draw_tokens(key, part):
    values = jnp.clip(jax.random.normal(key, (ROWS, D), jnp.float32), -6.0, 6.0)
    return values.astype(jnp.bfloat16)


def plant(entries, rng, low, largest):
    extent = entries.shape
    place = [jax.random.randint(jax.random.fold_in(rng, axis), (), 0, extent[axis]) for axis in range(len(extent))]
    entries = entries.at[tuple(place)].set(low)
    longest = extent.index(max(extent))
    place[longest] = (place[longest] + 1) % extent[longest]
    return entries.at[tuple(place)].set(largest)


def steps_of(key, dims, cuts, low, top_value):
    gain = 1.0
    for dim, blocks in cuts:
        steps = jax.random.uniform(jax.random.fold_in(jax.random.fold_in(key, 6), dim), (blocks,), jnp.float32, low / len(cuts), top_value / len(cuts))
        gain = gain * jnp.repeat(jnp.exp(steps), dims[dim] // blocks).reshape((-1,) + (1,) * (len(dims) - 1 - dim))
    return gain


def cumulative_ranks(count, skew):
    portions = [(1 << 20) // math.isqrt(standing ** skew) + 1 for standing in range(1, count + 1)]
    deviation = 1 + sum(portions) // (1 << 30)
    return np.cumsum(np.array([max(1, weight // deviation) for weight in portions]))


def ranked_ids(rng, extent, count, lean):
    grid = cumulative_ranks(count, lean)
    pick = jax.random.randint(jax.random.fold_in(rng, 1), extent, 0, int(grid[count - 1]))
    standing = jnp.searchsorted(jnp.asarray(grid, jnp.int32), pick, side="right")
    return jax.random.permutation(jax.random.fold_in(rng, 2), count)[standing].astype(jnp.int32)


def deal_out(key, own, number, rows, count, top, limit, lean):
    order = jax.random.permutation(key, count)
    crowded, ordinary = portions_of(count, rows * top, limit, lean, True), portions_of(count, rows * top, limit, lean, False)
    places = jnp.arange(count)

    def named(lengths, turn):
        used = int((lengths > 0).sum())
        fixed = max(1, used // 4)
        passed = fixed + (places - fixed + turn * (used - fixed)) % max(1, count - fixed)
        return jnp.zeros((count,), jnp.int32).at[order[jnp.where(places < fixed, places, passed)]].set(jnp.asarray(lengths, jnp.int32))

    lengths = jnp.where(number % 4 == 0, named(crowded, number // 4), named(ordinary, number - number // 4 - 1))
    mixed = jax.random.permutation(jax.random.fold_in(own, 3), count)
    donor, sink = mixed[0:count // 2 * 2:2], mixed[1:count // 2 * 2:2]
    room = jnp.minimum(lengths[donor] - 1, limit - lengths[sink]) // 2
    room = jnp.where((donor == order[0]) | (sink == order[0]) | (lengths[sink] == 0), 0, jnp.maximum(room, 0))
    passed = jax.random.randint(jax.random.fold_in(own, 4), (count // 2,), 0, 1 << 20) % (room + 1)
    lengths = lengths.at[donor].add(-passed).at[sink].add(passed)
    items = jnp.searchsorted(jnp.cumsum(lengths), jnp.arange(rows * top), side="right").astype(jnp.int32)
    listing = items.reshape(top, rows).T
    listing = listing[jax.random.permutation(jax.random.fold_in(own, 1), rows)]
    turn = jax.random.randint(jax.random.fold_in(own, 2), (rows, 1), 0, top)
    return jnp.take_along_axis(listing, (jnp.arange(top)[None, :] + turn) % top, axis=1)


def portions_of(count, total, limit, slope, full):
    portions = [(1 << 20) // math.isqrt(grade ** slope) + 1 for grade in range(1, count + 1)]
    largest = limit if full else min(limit, max(-(-total // count), total * portions[0] // sum(portions)))
    least = 1 if total - largest >= count - 1 else 0
    counts, surplus = [largest] + [least] * (count - 1), total - largest - least * (count - 1)
    while surplus > 0:
        movable = [i for i in range(1, count) if counts[i] < largest] or [i for i in range(1, count) if counts[i] < limit]
        pool, left = sum([portions[i] for i in movable]), surplus
        for i in movable:
            more = min(limit - counts[i], max(1, left * portions[i] // pool), surplus)
            counts[i] = counts[i] + more
            surplus = surplus - more
    return np.array(counts)


def gaussian(stream_key, extent, width, limit, shards=(), held_as=jnp.bfloat16):
    factor_of = steps_of(stream_key, extent, shards, -0.22, 0.18) if shards else 1.0
    drawn = jax.random.normal(stream_key, extent, jnp.float32) * width * factor_of
    return jnp.minimum(jnp.maximum(drawn, -limit), limit).astype(held_as)


def setup_inputs(seed: int = 0) -> dict:
    arg_keys = jax.random.split(jax.random.key(seed), 7)
    tokens = draw_tokens(jax.random.fold_in(arg_keys[6], 71), 0)
    owner_keys = jax.random.split(jax.random.fold_in(arg_keys[1], 1), ROWS // ROW_DEV)
    owner_turns = jax.random.permutation(jax.random.fold_in(arg_keys[1], 3), ROWS // ROW_DEV)
    owner = jax.vmap(lambda own, number: deal_out(jax.random.fold_in(arg_keys[1], 2), own, number, ROW_DEV, OWNERS, 1, CAP, 2))(owner_keys, owner_turns).reshape((ROWS, 1))
    list_local = plant(ranked_ids(arg_keys[2], (ROWS,), LIST_DEV, 2), jax.random.fold_in(arg_keys[2], 3), 0, LIST_DEV - 1).astype(jnp.int32)
    centroids = gaussian(arg_keys[3], (NLIST, D), 0.7, 5.0, ((0, 256),))
    rotation = gaussian(arg_keys[4], (D, D), D ** -0.5, 0.1875)
    codebook = gaussian(arg_keys[5], (M, DSUB, K), 1.2, 7.0, (), jnp.float32)
    return {"tokens": tokens, "owner": owner, "list_local": list_local, "centroids": centroids, "rotation": rotation, "codebook": codebook}


INV_TEMP = 0.2

def reference(tokens, owner, list_local, centroids, rotation, codebook):
    highest = lax.Precision.HIGHEST
    blocks = ROWS // ROW_DEV
    rep_index = jnp.arange(blocks, dtype=jnp.int32) % REPS
    owner_ids = owner[:, 0].reshape(blocks, ROW_DEV)
    list_ids = ((owner_ids * REPS + rep_index[:, None]) * LIST_DEV + list_local.reshape(blocks, ROW_DEV)).astype(jnp.int32)
    token_blocks = tokens.reshape(blocks, ROW_DEV, D)
    norms = lax.optimization_barrier(jnp.sum(codebook * codebook, axis=1))

    def one_block(carry, inputs):
        num_acc, cnt_acc, cross_acc = carry
        token_rows, row_lists = inputs
        centre_rows = jnp.take(centroids, row_lists, axis=0)
        residual = (token_rows.astype(jnp.float32) - centre_rows.astype(jnp.float32)).astype(jnp.bfloat16)
        rotated = jnp.dot(residual, rotation, preferred_element_type=jnp.float32).reshape(ROW_DEV, M, DSUB)
        logits = (2.0 * jnp.einsum('smj,mjk->smk', rotated, codebook, precision=highest) - norms[None]) * INV_TEMP
        prob = jax.nn.softmax(logits, axis=-1)
        num = jnp.einsum('smk,smj->mjk', prob, rotated, precision=highest)
        cnt = lax.optimization_barrier(jnp.sum(prob, axis=0))
        rebuilt = jnp.einsum('smk,mjk->smj', prob, codebook, precision=highest).reshape(ROW_DEV, D).astype(jnp.bfloat16)
        cross = lax.dot_general(residual, rebuilt, (((0,), (0,)), ((), ())), preferred_element_type=jnp.float32)
        return ((num_acc + num, cnt_acc + cnt, cross_acc + cross), None)
    start = (jnp.zeros((M, DSUB, K), jnp.float32), jnp.zeros((M, K), jnp.float32), jnp.zeros((D, D), jnp.float32))
    result = lax.scan(one_block, start, (token_blocks, list_ids))
    totals = result[0]
    new_codebook = (totals[0] + codebook) / (totals[1][:, None, :] + 1.0)
    cross_cov = totals[2] * (1.0 / math.sqrt(ROWS))
    return (new_codebook, cross_cov)
```

```python
import math

import jax
import jax.numpy as jnp
from jax import lax
from jax.experimental import pallas as pl
from jax.experimental.pallas import tpu as pltpu
from jax.sharding import Mesh
from jax.sharding import PartitionSpec as P

ALL = ("x", "c", "z", "y")
GRP = ("x", "c")
OWNERS = 8
CAP = 128
LISTS = 1024
ROWS = 512
D = 1024
M = 16
DSUB = 64
K = 256
WIDE = D + 2 * K
INV_TEMP = 0.2
F32 = jnp.float32
BF16 = jnp.bfloat16


def dot(a, b, ca=1, cb=0):
    return lax.dot_general(a, b, (((ca,), (cb,)), ((), ())), preferred_element_type=F32)


def iota(shape, dim):
    return lax.broadcasted_iota(jnp.int32, shape, dim)


def one_hot(hit):
    return jnp.where(hit, 1.0, 0.0).astype(BF16)


def slots_kernel(owner_ref, lists_ref, slot_ref, ids_ref):
    owner = owner_ref[...]
    mine = owner == iota((ROWS, 128), 1)
    earlier = one_hot(iota((ROWS, ROWS), 0) > iota((ROWS, ROWS), 1))
    before = dot(earlier, one_hot(mine))
    position = jnp.sum(jnp.where(mine, before, 0.0), axis=1, keepdims=True)
    slot = owner * CAP + position.astype(jnp.int32)
    slot_ref[...] = slot
    lists = lists_ref[...]
    row = iota((8, ROWS), 0)
    parts = jnp.where(row == 0, lists >> 5, jnp.where(row == 1, lists & 31, 1))
    sent = dot(parts.astype(F32).astype(BF16), one_hot(slot == iota((ROWS, OWNERS * CAP), 1)))
    ids = sent[0:1] * 32.0 + sent[1:2] + sent[2:3] - 1.0
    for o in range(OWNERS):
        ids_ref[o : o + 1, :] = ids[:, o * CAP : (o + 1) * CAP].astype(jnp.int32)


def centres_kernel(ids_ref, centroids_ref, out_ref):
    ids = ids_ref[...].astype(F32).T.astype(jnp.int32)
    table = centroids_ref[...]
    for s in range(OWNERS):
        pick = one_hot(ids[:, s : s + 1] == iota((CAP, LISTS), 1))
        out_ref[s] = dot(pick, table).astype(BF16)


def codes_kernel(book_ref, stack_ref, turned_ref, norm_ref):
    for i in range(4):
        book = book_ref[i]
        high = book.astype(BF16)
        low = (book - high.astype(F32)).astype(BF16)
        stack_ref[i] = jnp.concatenate([high, low, high, low], axis=0)
        turned = jnp.concatenate([high.astype(F32), low.astype(F32)], axis=0).T
        turned_ref[i] = turned.astype(BF16)
        norm_ref[i] = INV_TEMP * jnp.sum(book * book, axis=0, keepdims=True)


def stats_kernel(
    tokens_ref, slot_ref, got_ref, rotation_ref, stack_ref, turned_ref, norm_ref,
    out_ref, res_ref, turned_res_ref,
):
    step = pl.program_id(0)

    @pl.when(step == 0)
    def _():
        pick = one_hot(slot_ref[...] == iota((ROWS, OWNERS * CAP), 1))
        centres = dot(pick, got_ref[...])
        res = (tokens_ref[...].astype(F32) - centres).astype(BF16)
        res_ref[...] = res
        d = iota((D, D), 1)
        place = (
            ((d >> 7) & 1) * 512 + (d >> 8) * 128 + ((d >> 2) & 3) * 32 + ((d >> 4) & 7) * 4
        ) + (d & 3)
        turned_res_ref[...] = dot(one_hot(iota((D, D), 0) == place), res, 1, 1).astype(BF16)

    rotated = dot(res_ref[...], rotation_ref[...])
    left = iota((ROWS, 2 * DSUB), 1) < DSUB
    pieces = []
    for pair in range(2):
        both = rotated[:, pair * 128 : (pair + 1) * 128]
        swapped = pltpu.roll(both, DSUB, 1)
        halves = []
        for side in range(2):
            m = 2 * pair + side
            twice = jnp.where(left, both, swapped) if side == 0 else jnp.where(left, swapped, both)
            high = twice.astype(BF16)
            rest = twice - high.astype(F32)
            low = rest.astype(BF16)
            logits = (2.0 * INV_TEMP) * dot(jnp.concatenate([high, low], axis=1), stack_ref[m]) - norm_ref[m]
            power = jnp.exp(logits - jnp.max(logits, axis=1, keepdims=True))
            prob = power * (1.0 / jnp.sum(power, axis=1, keepdims=True))
            mass = jnp.sum(prob, axis=0, keepdims=True)
            prob = prob.astype(BF16)
            split = jnp.where(left, high.astype(F32), rest).astype(BF16)
            num = dot(split, prob, 0, 0)
            at = pl.ds(pl.multiple_of(step * 256 + m * DSUB, DSUB), DSUB)
            out_ref[at, D : D + K] = (num[:DSUB] + num[DSUB:]).astype(BF16)
            out_ref[at, D + K : D + 2 * K] = jnp.broadcast_to(mass, (DSUB, K)).astype(BF16)
            back = dot(prob, turned_ref[m])
            halves.append(back + pltpu.roll(back, DSUB, 1))
        pieces.append(jnp.where(left, halves[0], halves[1]).astype(BF16))
    cross = dot(turned_res_ref[...], jnp.concatenate(pieces, axis=1)).astype(BF16)
    for q in range(4):
        @pl.when(step == q)
        def _():
            out_ref[:, q * 256 : (q + 1) * 256] = cross


def whole(shape):
    return pl.BlockSpec(shape, lambda *_: (0,) * len(shape))


def find_slots(owner, lists):
    return pl.pallas_call(
        slots_kernel,
        out_shape=(
            jax.ShapeDtypeStruct((ROWS, 1), jnp.int32),
            jax.ShapeDtypeStruct((OWNERS, CAP), jnp.int32),
        ),
        name="slots",
    )(owner, lists.reshape(1, ROWS))


def find_centres(ids, centroids):
    return pl.pallas_call(
        centres_kernel,
        out_shape=jax.ShapeDtypeStruct((OWNERS, CAP, D), BF16),
        name="centres",
    )(ids, centroids)


def split_codes(codebook):
    def block(*shape):
        return pl.BlockSpec((4, *shape), lambda i: (i, 0, 0))

    return pl.pallas_call(
        codes_kernel,
        grid=(M // 4,),
        in_specs=[block(DSUB, K)],
        out_specs=(block(4 * DSUB, K), block(K, 2 * DSUB), block(1, K)),
        out_shape=(
            jax.ShapeDtypeStruct((M, 4 * DSUB, K), BF16),
            jax.ShapeDtypeStruct((M, K, 2 * DSUB), BF16),
            jax.ShapeDtypeStruct((M, 1, K), F32),
        ),
        name="codes",
    )(codebook)


def code_stats(tokens, slot, got, rotation, codes):
    def block(*shape):
        return pl.BlockSpec((4, *shape), lambda i: (i, 0, 0))

    return pl.pallas_call(
        stats_kernel,
        grid=(M // 4,),
        in_specs=[
            whole((ROWS, D)),
            whole((ROWS, 1)),
            whole((OWNERS * CAP, D)),
            pl.BlockSpec((D, 256), lambda i: (0, i)),
            block(4 * DSUB, K),
            block(K, 2 * DSUB),
            block(1, K),
        ],
        out_specs=whole((D, WIDE)),
        out_shape=jax.ShapeDtypeStruct((D, WIDE), BF16),
        scratch_shapes=[pltpu.VMEM((ROWS, D), BF16), pltpu.VMEM((D, ROWS), BF16)],
        name="stats",
    )(tokens, slot, got, rotation, *codes)


def swap(value, axis):
    return lax.all_to_all(value, axis, split_axis=0, concat_axis=0, tiled=True)


def sent_to_all(value, axis):
    copies = jnp.broadcast_to(value, (lax.axis_size(axis), *value.shape))
    return swap(copies, axis).reshape(-1, value.shape[-1])


def local(tokens, owner, list_local, centroids, rotation, codebook):
    slot, ids = find_slots(owner, list_local)
    centres = find_centres(swap(ids, GRP), centroids)
    got = swap(centres, GRP).reshape(OWNERS * CAP, D)
    part = code_stats(tokens, slot, got, rotation, split_codes(codebook))
    part = swap(part.reshape(2, 512, WIDE), "c").astype(F32).sum(axis=0).astype(BF16)
    part = swap(part.reshape(16, 32, WIDE), ("x", "y")).astype(F32).sum(axis=0)
    part = swap(part.reshape(8, 4, WIDE), "z").sum(axis=0)
    cross_cov = part[:, :D] * (1.0 / math.sqrt(ROWS * 256))
    place = (lax.axis_index("c") * 16 + lax.axis_index(("x", "y"))) * 8 + lax.axis_index("z")
    book = lax.dynamic_slice_in_dim(codebook.reshape(M * DSUB, K), place * 4, 4, 0)
    fresh = (part[:, D : D + K] + book) / (part[:, D + K :] + 1.0)
    fresh = sent_to_all(sent_to_all(sent_to_all(fresh, "z"), ("x", "y")), "c")
    return (fresh.reshape(M, DSUB, K), cross_cov)


def solution(mesh):
    finer = Mesh(mesh.devices.reshape(4, 2, 8, 4), ALL)
    in_specs = (P(ALL, None), P(ALL, None), P(ALL), P(ALL, None), P(), P())
    out_specs = (P(), P(ALL, None))
    return jax.shard_map(local, mesh=finer, in_specs=in_specs, out_specs=out_specs, check_vma=False)
```

```python
import math

import jax
import jax.numpy as jnp
from jax import lax
from jax.experimental import pallas as pl
from jax.experimental.pallas import tpu as pltpu
from jax.sharding import Mesh
from jax.sharding import PartitionSpec as P

ALL = ("x", "c", "z", "y")
GRP = ("x", "c")
XY = ("x", "y")
OWNERS = 8
CAP = 128
LISTS = 1024
ROWS = 512
D = 1024
M = 16
DSUB = 64
K = 256
WIDE = D + K + 128
INV_TEMP = 0.2
F32 = jnp.float32
BF16 = jnp.bfloat16


def dot(a, b, ca=1, cb=0):
    return lax.dot_general(a, b, (((ca,), (cb,)), ((), ())), preferred_element_type=F32)


def iota(shape, dim):
    return lax.broadcasted_iota(jnp.int32, shape, dim)


def one_hot(hit):
    return jnp.where(hit, 1.0, 0.0).astype(BF16)


def slots_kernel(owner_ref, lists_ref, slot_ref, ids_ref):
    owner = owner_ref[...]
    mine = owner == iota((ROWS, 128), 1)
    earlier = one_hot(iota((ROWS, ROWS), 0) > iota((ROWS, ROWS), 1))
    before = dot(earlier, one_hot(mine))
    position = jnp.sum(jnp.where(mine, before, 0.0), axis=1, keepdims=True)
    slot = owner * CAP + position.astype(jnp.int32)
    slot_ref[...] = slot
    lists = lists_ref[...]
    row = iota((8, ROWS), 0)
    parts = jnp.where(row == 0, lists >> 5, jnp.where(row == 1, lists & 31, 1))
    sent = dot(parts.astype(F32).astype(BF16), one_hot(slot == iota((ROWS, OWNERS * CAP), 1)))
    ids = sent[0:1] * 32.0 + sent[1:2] + sent[2:3] - 1.0
    for o in range(OWNERS):
        ids_ref[o : o + 1, :] = ids[:, o * CAP : (o + 1) * CAP].astype(jnp.int32)


def centres_kernel(ids_ref, centroids_ref, out_ref):
    ids = ids_ref[...].astype(F32).T.astype(jnp.int32)
    table = centroids_ref[...]
    for s in range(OWNERS):
        pick = one_hot(ids[:, s : s + 1] == iota((CAP, LISTS), 1))
        out_ref[s] = dot(pick, table).astype(BF16)


def codes_kernel(book_ref, stack_ref, turned_ref, norm_ref):
    for i in range(4):
        book = book_ref[i]
        high = book.astype(BF16)
        low = (book - high.astype(F32)).astype(BF16)
        stack_ref[i] = jnp.concatenate([high, low, high, low], axis=0)
        turned = jnp.concatenate([high.astype(F32), low.astype(F32)], axis=0).T
        turned_ref[i] = turned.astype(BF16)
        norm_ref[i] = INV_TEMP * jnp.sum(book * book, axis=0, keepdims=True)


def stats_kernel(
    tokens_ref, slot_ref, got_ref, rotation_ref, stack_ref, turned_ref, norm_ref,
    out_ref, res_ref, turned_res_ref,
):
    step = pl.program_id(0)

    @pl.when(step == 0)
    def _():
        pick = one_hot(slot_ref[...] == iota((ROWS, OWNERS * CAP), 1))
        centres = dot(pick, got_ref[...])
        res = (tokens_ref[...].astype(F32) - centres).astype(BF16)
        res_ref[...] = res
        d = iota((D, D), 1)
        place = (
            ((d >> 7) & 1) * 512 + (d >> 8) * 128 + ((d >> 2) & 3) * 32 + ((d >> 4) & 7) * 4
        ) + (d & 3)
        turned_res_ref[...] = dot(one_hot(iota((D, D), 0) == place), res, 1, 1).astype(BF16)

    rotated = dot(res_ref[...], rotation_ref[...])
    left = iota((ROWS, 2 * DSUB), 1) < DSUB
    pieces = []
    for pair in range(2):
        both = rotated[:, pair * 128 : (pair + 1) * 128]
        swapped = pltpu.roll(both, DSUB, 1)
        halves = []
        for side in range(2):
            m = 2 * pair + side
            twice = jnp.where(left, both, swapped) if side == 0 else jnp.where(left, swapped, both)
            high = twice.astype(BF16)
            rest = twice - high.astype(F32)
            low = rest.astype(BF16)
            logits = (2.0 * INV_TEMP) * dot(jnp.concatenate([high, low], axis=1), stack_ref[m]) - norm_ref[m]
            power = jnp.exp(logits - jnp.max(logits, axis=1, keepdims=True))
            prob = power * (1.0 / jnp.sum(power, axis=1, keepdims=True))
            mass = jnp.sum(prob, axis=0, keepdims=True)
            prob = prob.astype(BF16)
            split = jnp.where(left, high.astype(F32), rest).astype(BF16)
            num = dot(split, prob, 0, 0)
            at = pl.ds(pl.multiple_of(step * 256 + m * DSUB, DSUB), DSUB)
            out_ref[at, D : D + K] = (num[:DSUB] + num[DSUB:]).astype(BF16)
            row = iota((DSUB, 128), 0) % 32
            masses = jnp.where(row == 0, mass[:, :128], jnp.where(row == 1, mass[:, 128:], 0.0))
            out_ref[at, D + K :] = masses.astype(BF16)
            back = dot(prob, turned_ref[m])
            halves.append(back + pltpu.roll(back, DSUB, 1))
        pieces.append(jnp.where(left, halves[0], halves[1]).astype(BF16))
    cross = dot(turned_res_ref[...], jnp.concatenate(pieces, axis=1)).astype(BF16)
    for q in range(4):
        @pl.when(step == q)
        def _():
            out_ref[:, q * 256 : (q + 1) * 256] = cross


def pack_kernel(part_ref, out_ref):
    total = part_ref[0].astype(F32)
    for i in range(1, 16):
        total = total + part_ref[i].astype(F32)
    mass = jnp.concatenate([total[0:1, D + K :], total[1:2, D + K :], jnp.zeros((1, D - K), F32)], axis=1)
    mass = jnp.broadcast_to(mass, (4, D))
    num = jnp.concatenate([total[8 * b : 8 * b + 8, D : D + K] for b in range(4)], axis=1)
    for z in range(8):
        head = jnp.concatenate([total[4 * z : 4 * z + 4, :D], mass], axis=0)
        out_ref[z] = jnp.concatenate([head, num], axis=0).astype(BF16)


def finish_kernel(part_ref, book_ref, cross_ref, fresh_ref):
    total = part_ref[0].astype(F32)
    for i in range(1, 8):
        total = total + part_ref[i].astype(F32)
    cross_ref[...] = total[0:4] * (1.0 / math.sqrt(ROWS * 256))
    count = total[4:5, :K] + 1.0
    for b in range(4):
        at = slice(8 * b, 8 * b + 8)
        fresh_ref[at] = (total[8:16, b * K : (b + 1) * K] + book_ref[at]) / count


def pack(part):
    return pl.pallas_call(
        pack_kernel, out_shape=jax.ShapeDtypeStruct((8, 16, D), BF16), name="pack"
    )(part)


def finish(part, book):
    return pl.pallas_call(
        finish_kernel,
        out_shape=(jax.ShapeDtypeStruct((4, D), F32), jax.ShapeDtypeStruct((32, K), F32)),
        name="finish",
    )(part, book)


def whole(shape):
    return pl.BlockSpec(shape, lambda *_: (0,) * len(shape))


def find_slots(owner, lists):
    return pl.pallas_call(
        slots_kernel,
        out_shape=(
            jax.ShapeDtypeStruct((ROWS, 1), jnp.int32),
            jax.ShapeDtypeStruct((OWNERS, CAP), jnp.int32),
        ),
        name="slots",
    )(owner, lists.reshape(1, ROWS))


def find_centres(ids, centroids):
    return pl.pallas_call(
        centres_kernel,
        out_shape=jax.ShapeDtypeStruct((OWNERS, CAP, D), BF16),
        name="centres",
    )(ids, centroids)


def split_codes(codebook):
    def block(*shape):
        return pl.BlockSpec((4, *shape), lambda i: (i, 0, 0))

    return pl.pallas_call(
        codes_kernel,
        grid=(M // 4,),
        in_specs=[block(DSUB, K)],
        out_specs=(block(4 * DSUB, K), block(K, 2 * DSUB), block(1, K)),
        out_shape=(
            jax.ShapeDtypeStruct((M, 4 * DSUB, K), BF16),
            jax.ShapeDtypeStruct((M, K, 2 * DSUB), BF16),
            jax.ShapeDtypeStruct((M, 1, K), F32),
        ),
        name="codes",
    )(codebook)


def code_stats(tokens, slot, got, rotation, codes):
    def block(*shape):
        return pl.BlockSpec((4, *shape), lambda i: (i, 0, 0))

    return pl.pallas_call(
        stats_kernel,
        grid=(M // 4,),
        in_specs=[
            whole((ROWS, D)),
            whole((ROWS, 1)),
            whole((OWNERS * CAP, D)),
            pl.BlockSpec((D, 256), lambda i: (0, i)),
            block(4 * DSUB, K),
            block(K, 2 * DSUB),
            block(1, K),
        ],
        out_specs=whole((D, WIDE)),
        out_shape=jax.ShapeDtypeStruct((D, WIDE), BF16),
        scratch_shapes=[pltpu.VMEM((ROWS, D), BF16), pltpu.VMEM((D, ROWS), BF16)],
        name="stats",
    )(tokens, slot, got, rotation, *codes)


def swap(value, axis):
    return lax.all_to_all(value, axis, split_axis=0, concat_axis=0, tiled=True)


def sent_to_all(value, axis):
    copies = jnp.broadcast_to(value, (lax.axis_size(axis), *value.shape))
    return swap(copies, axis).reshape(-1, value.shape[-1])


def local(tokens, owner, list_local, centroids, rotation, codebook):
    slot, ids = find_slots(owner, list_local)
    centres = find_centres(swap(ids, GRP), centroids)
    got = swap(centres, GRP).reshape(OWNERS * CAP, D)
    part = code_stats(tokens, slot, got, rotation, split_codes(codebook))
    part = swap(part.reshape(2, 512, WIDE), "c").astype(F32).sum(axis=0).astype(BF16)
    part = swap(pack(swap(part.reshape(16, 32, WIDE), XY)), "z")
    place = lax.axis_index("c") * 16 + lax.axis_index(XY)
    book = lax.dynamic_slice_in_dim(codebook.reshape(M * DSUB, K), place * 32, 32, 0)
    cross_cov, fresh = finish(part, book)
    fresh = sent_to_all(sent_to_all(fresh, XY), "c")
    return (fresh.reshape(M, DSUB, K), cross_cov)


def solution(mesh):
    finer = Mesh(mesh.devices.reshape(4, 2, 8, 4), ALL)
    in_specs = (P(ALL, None), P(ALL, None), P(ALL), P(ALL, None), P(), P())
    out_specs = (P(), P(ALL, None))
    return jax.shard_map(local, mesh=finer, in_specs=in_specs, out_specs=out_specs, check_vma=False)
```

```python
import math
from functools import partial

import jax
import jax.numpy as jnp
from jax import lax
from jax.experimental import pallas as pl
from jax.experimental.pallas import tpu as pltpu
from jax.sharding import Mesh
from jax.sharding import PartitionSpec as P

ALL = ("x", "c", "z", "y")
GRP = ("x", "c")
XY = ("x", "y")
OWNERS = 8
CAP = 128
LISTS = 1024
ROWS = 512
HALF = 256
SLOTS = 512
D = 1024
M = 16
DSUB = 64
K = 256
WIDE = D + K + 128
INV_TEMP = 0.2
F32 = jnp.float32
BF16 = jnp.bfloat16


def dot(a, b, ca=1, cb=0):
    return lax.dot_general(a, b, (((ca,), (cb,)), ((), ())), preferred_element_type=F32)


def iota(shape, dim):
    return lax.broadcasted_iota(jnp.int32, shape, dim)


def one_hot(hit):
    return jnp.where(hit, 1.0, 0.0).astype(BF16)


def as_row(column):
    return jnp.broadcast_to(column, (ROWS, 128)).T[0:1]


def slots_kernel(owner_ref, lists_ref, slot_ref, rank_ref, ids_ref):
    owner = owner_ref[...]
    mine = owner == iota((ROWS, 128), 1)
    earlier = one_hot(iota((ROWS, ROWS), 0) > iota((ROWS, ROWS), 1))
    before = dot(earlier, one_hot(mine))
    position = jnp.sum(jnp.where(mine, before, 0.0), axis=1, keepdims=True)
    lists = lists_ref[...]
    row = iota((8, ROWS), 0)
    parts = jnp.where(row == 0, lists >> 5, jnp.where(row == 1, lists & 31, 1))
    target = owner * CAP + position.astype(jnp.int32)
    sent = dot(parts.astype(F32).astype(BF16), one_hot(target == iota((ROWS, OWNERS * CAP), 1)))
    ids = sent[0:1] * 32.0 + sent[1:2] + sent[2:3] - 1.0
    for o in range(OWNERS):
        ids_ref[o : o + 1, :] = ids[:, o * CAP : (o + 1) * CAP].astype(jnp.int32)
    key = position * ROWS + iota((ROWS, 1), 0).astype(F32)
    lower = jnp.where(jnp.broadcast_to(key, (ROWS, ROWS)) < as_row(key), 1.0, 0.0)
    rank_ref[...] = jnp.sum(lower, axis=0, keepdims=True).astype(jnp.int32)
    late = jnp.where(position >= 64.0, SLOTS - 64.0, 0.0)
    slot = owner.astype(F32) * 64.0 + position + late
    slot_ref[...] = as_row(slot).astype(jnp.int32)


def centres_kernel(half, ids_ref, centroids_ref, out_ref):
    ids = ids_ref[...].astype(F32).T.astype(jnp.int32)
    table = centroids_ref[...]
    for s in range(OWNERS):
        mine = ids[half * 64 : half * 64 + 64, s : s + 1]
        out_ref[s] = dot(one_hot(mine == iota((64, LISTS), 1)), table).astype(BF16)


def codes_kernel(book_ref, stack_ref, turned_ref, norm_ref):
    for i in range(4):
        book = book_ref[i]
        high = book.astype(BF16)
        low = (book - high.astype(F32)).astype(BF16)
        stack_ref[i] = jnp.concatenate([high, low, high, low], axis=0)
        turned = jnp.concatenate([high.astype(F32), low.astype(F32)], axis=0).T
        turned_ref[i] = turned.astype(BF16)
        norm_ref[i] = INV_TEMP * jnp.sum(book * book, axis=0, keepdims=True)


def residuals(half, tokens_ref, rank_ref, slot_ref, gots):
    chosen = rank_ref[...] == iota((HALF, ROWS), 0) + half * HALF
    rows = dot(one_hot(chosen), tokens_ref[...])
    slot = jnp.sum(jnp.where(chosen, slot_ref[...], 0), axis=1, keepdims=True)
    centres = jnp.zeros((HALF, D), F32)
    for i, got_ref in enumerate(gots):
        centres += dot(one_hot(slot == iota((HALF, SLOTS), 1) + i * SLOTS), got_ref[...])
    return (rows - centres).astype(BF16)


def turned_and_placed(res):
    d = iota((D, D), 1)
    place = (
        ((d >> 7) & 1) * 512 + (d >> 8) * 128 + ((d >> 2) & 3) * 32 + ((d >> 4) & 7) * 4
    ) + (d & 3)
    return dot(one_hot(iota((D, D), 0) == place), res, 1, 1).astype(BF16)


def four_codes(res_ref, rotation_ref, stack_ref, turned_ref, norm_ref, write):
    rotated = dot(res_ref[...], rotation_ref[...])
    left = iota((HALF, 2 * DSUB), 1) < DSUB
    pieces = []
    for pair in range(2):
        both = rotated[:, pair * 128 : (pair + 1) * 128]
        swapped = pltpu.roll(both, DSUB, 1)
        halves = []
        for side in range(2):
            m = 2 * pair + side
            twice = jnp.where(left, both, swapped) if side == 0 else jnp.where(left, swapped, both)
            high = twice.astype(BF16)
            rest = twice - high.astype(F32)
            low = rest.astype(BF16)
            logits = (2.0 * INV_TEMP) * dot(jnp.concatenate([high, low], axis=1), stack_ref[m]) - norm_ref[m]
            power = jnp.exp(logits - jnp.max(logits, axis=1, keepdims=True))
            prob = power * (1.0 / jnp.sum(power, axis=1, keepdims=True))
            mass = jnp.sum(prob, axis=0, keepdims=True)
            prob = prob.astype(BF16)
            split = jnp.where(left, high.astype(F32), rest).astype(BF16)
            num = dot(split, prob, 0, 0)
            row = iota((DSUB, 128), 0) % 32
            masses = jnp.where(row == 0, mass[:, :128], jnp.where(row == 1, mass[:, 128:], 0.0))
            at = pl.ds(pl.multiple_of(pl.program_id(0) * 256 + m * DSUB, DSUB), DSUB)
            write(at, num[:DSUB] + num[DSUB:], masses)
            back = dot(prob, turned_ref[m])
            halves.append(back + pltpu.roll(back, DSUB, 1))
        pieces.append(jnp.where(left, halves[0], halves[1]).astype(BF16))
    return jnp.concatenate(pieces, axis=1)


def first_stats_kernel(
    tokens_ref, rank_ref, slot_ref, early_ref, rotation_ref, stack_ref, turned_ref, norm_ref,
    num_ref, back_ref, placed_ref, res_ref,
):
    @pl.when(pl.program_id(0) == 0)
    def _():
        res = residuals(0, tokens_ref, rank_ref, slot_ref, (early_ref,))
        res_ref[...] = res
        placed_ref[...] = turned_and_placed(res)

    def write(at, num, masses):
        num_ref[at, :K] = num
        num_ref[at, K:] = masses

    back_ref[...] = four_codes(res_ref, rotation_ref, stack_ref, turned_ref, norm_ref, write)


def second_stats_kernel(
    tokens_ref, rank_ref, slot_ref, early_ref, late_ref, rotation_ref, stack_ref, turned_ref, norm_ref,
    num_ref, back_ref, placed_ref, out_ref, res_ref, placed_too_ref,
):
    step = pl.program_id(0)

    @pl.when(step == 0)
    def _():
        res = residuals(1, tokens_ref, rank_ref, slot_ref, (early_ref, late_ref))
        res_ref[...] = res
        placed_too_ref[...] = turned_and_placed(res)

    def write(at, num, masses):
        out_ref[at, D : D + K] = (num + num_ref[at, :K]).astype(BF16)
        out_ref[at, D + K :] = (masses + num_ref[at, K:]).astype(BF16)

    back = four_codes(res_ref, rotation_ref, stack_ref, turned_ref, norm_ref, write)
    cross = dot(placed_ref[...], back_ref[...]) + dot(placed_too_ref[...], back)
    cross = cross.astype(BF16)
    for q in range(4):
        @pl.when(step == q)
        def _():
            out_ref[:, q * 256 : (q + 1) * 256] = cross


def pack_kernel(part_ref, out_ref):
    total = part_ref[0].astype(F32)
    for i in range(1, 16):
        total = total + part_ref[i].astype(F32)
    mass = jnp.concatenate([total[0:1, D + K :], total[1:2, D + K :], jnp.zeros((1, D - K), F32)], axis=1)
    mass = jnp.broadcast_to(mass, (4, D))
    num = jnp.concatenate([total[8 * b : 8 * b + 8, D : D + K] for b in range(4)], axis=1)
    for z in range(8):
        head = jnp.concatenate([total[4 * z : 4 * z + 4, :D], mass], axis=0)
        out_ref[z] = jnp.concatenate([head, num], axis=0)


def finish_kernel(part_ref, book_ref, cross_ref, fresh_ref):
    total = part_ref[0]
    for i in range(1, 8):
        total = total + part_ref[i]
    cross_ref[...] = total[0:4] * (1.0 / math.sqrt(ROWS * 256))
    count = total[4:5, :K] + 1.0
    for b in range(4):
        at = slice(8 * b, 8 * b + 8)
        fresh_ref[at] = (total[8:16, b * K : (b + 1) * K] + book_ref[at]) / count


def pack(part):
    return pl.pallas_call(
        pack_kernel, out_shape=jax.ShapeDtypeStruct((8, 16, D), F32), name="pack"
    )(part)


def finish(part, book):
    return pl.pallas_call(
        finish_kernel,
        out_shape=(jax.ShapeDtypeStruct((4, D), F32), jax.ShapeDtypeStruct((32, K), F32)),
        name="finish",
    )(part, book)


def whole(shape):
    return pl.BlockSpec(shape, lambda *_: (0,) * len(shape))


def find_slots(owner, lists):
    line = jax.ShapeDtypeStruct((1, ROWS), jnp.int32)
    return pl.pallas_call(
        slots_kernel,
        out_shape=(line, line, jax.ShapeDtypeStruct((OWNERS, CAP), jnp.int32)),
        name="slots",
    )(owner, lists.reshape(1, ROWS))


def find_centres(half, ids, centroids):
    return pl.pallas_call(
        partial(centres_kernel, half),
        out_shape=jax.ShapeDtypeStruct((OWNERS, 64, D), BF16),
        name="centres",
    )(ids, centroids)


def split_codes(codebook):
    def block(*shape):
        return pl.BlockSpec((4, *shape), lambda i: (i, 0, 0))

    return pl.pallas_call(
        codes_kernel,
        grid=(M // 4,),
        in_specs=[block(DSUB, K)],
        out_specs=(block(4 * DSUB, K), block(K, 2 * DSUB), block(1, K)),
        out_shape=(
            jax.ShapeDtypeStruct((M, 4 * DSUB, K), BF16),
            jax.ShapeDtypeStruct((M, K, 2 * DSUB), BF16),
            jax.ShapeDtypeStruct((M, 1, K), F32),
        ),
        name="codes",
    )(codebook)


def code_stats(rows, gots, rotation, codes, before=()):
    def block(*shape):
        return pl.BlockSpec((4, *shape), lambda i: (i, 0, 0))

    columns = pl.BlockSpec((HALF, 256), lambda i: (0, i))
    sums = [whole((D, K + 128)), columns, whole((D, HALF))]
    placed = pltpu.VMEM((D, HALF), BF16)
    first = not before
    shapes = (
        jax.ShapeDtypeStruct((D, K + 128), F32),
        jax.ShapeDtypeStruct((HALF, D), BF16),
        jax.ShapeDtypeStruct((D, HALF), BF16),
    )
    return pl.pallas_call(
        first_stats_kernel if first else second_stats_kernel,
        grid=(M // 4,),
        in_specs=[
            whole((ROWS, D)),
            whole((1, ROWS)),
            whole((1, ROWS)),
            *[whole((SLOTS, D)) for _ in gots],
            pl.BlockSpec((D, 256), lambda i: (0, i)),
            block(4 * DSUB, K),
            block(K, 2 * DSUB),
            block(1, K),
            *([] if first else sums),
        ],
        out_specs=tuple(sums) if first else whole((D, WIDE)),
        out_shape=shapes if first else jax.ShapeDtypeStruct((D, WIDE), BF16),
        scratch_shapes=[pltpu.VMEM((HALF, D), BF16)] + ([] if first else [placed]),
        name="first_stats" if first else "second_stats",
    )(*rows, *gots, rotation, *codes, *before)


def swap(value, axis):
    return lax.all_to_all(value, axis, split_axis=0, concat_axis=0, tiled=True)


def sent_to_all(value, axis):
    copies = jnp.broadcast_to(value, (lax.axis_size(axis), *value.shape))
    return swap(copies, axis).reshape(-1, value.shape[-1])


def local(tokens, owner, list_local, centroids, rotation, codebook):
    slot, rank, ids = find_slots(owner, list_local)
    ids = swap(ids, GRP)
    early = swap(find_centres(0, ids, centroids), GRP).reshape(SLOTS, D)
    late = swap(find_centres(1, ids, centroids), GRP).reshape(SLOTS, D)
    rows = (tokens, rank, slot)
    codes = split_codes(codebook)
    before = code_stats(rows, (early,), rotation, codes)
    part = code_stats(rows, (early, late), rotation, codes, before)
    part = swap(part.reshape(2, 512, WIDE), "c").astype(F32).sum(axis=0).astype(BF16)
    part = swap(pack(swap(part.reshape(16, 32, WIDE), XY)), "z")
    place = lax.axis_index("c") * 16 + lax.axis_index(XY)
    book = lax.dynamic_slice_in_dim(codebook.reshape(M * DSUB, K), place * 32, 32, 0)
    cross_cov, fresh = finish(part, book)
    fresh = sent_to_all(sent_to_all(fresh, XY), "c")
    return (fresh.reshape(M, DSUB, K), cross_cov)


def solution(mesh):
    finer = Mesh(mesh.devices.reshape(4, 2, 8, 4), ALL)
    in_specs = (P(ALL, None), P(ALL, None), P(ALL), P(ALL, None), P(), P())
    out_specs = (P(), P(ALL, None))
    return jax.shard_map(local, mesh=finer, in_specs=in_specs, out_specs=out_specs, check_vma=False)
```

```python
import math

import jax
import jax.numpy as jnp
from jax import lax
from jax.experimental import pallas as pl
from jax.experimental.pallas import tpu as pltpu
from jax.sharding import Mesh
from jax.sharding import PartitionSpec as P

ALL = ("x", "c", "z", "y")
GRP = ("x", "c")
XY = ("x", "y")
OWNERS = 8
CAP = 128
LISTS = 1024
ROWS = 512
D = 1024
M = 16
DSUB = 64
K = 256
WIDE = D + K + 128
INV_TEMP = 0.2
F32 = jnp.float32
BF16 = jnp.bfloat16


def dot(a, b, ca=1, cb=0):
    return lax.dot_general(a, b, (((ca,), (cb,)), ((), ())), preferred_element_type=F32)


def iota(shape, dim):
    return lax.broadcasted_iota(jnp.int32, shape, dim)


def one_hot(hit):
    return jnp.where(hit, 1.0, 0.0).astype(BF16)


def slots_kernel(owner_ref, lists_ref, slot_ref, ids_ref):
    owner = jnp.broadcast_to(owner_ref[...].astype(F32), (128, ROWS)).T[:, 0:1].astype(jnp.int32)
    mine = owner == iota((ROWS, 128), 1)
    earlier = one_hot(iota((ROWS, ROWS), 0) > iota((ROWS, ROWS), 1))
    before = dot(earlier, one_hot(mine))
    position = jnp.sum(jnp.where(mine, before, 0.0), axis=1, keepdims=True)
    slot = owner * CAP + position.astype(jnp.int32)
    slot_ref[...] = slot
    lists = lists_ref[...]
    row = iota((8, ROWS), 0)
    parts = jnp.where(row == 0, lists >> 5, jnp.where(row == 1, lists & 31, 1))
    sent = dot(parts.astype(F32).astype(BF16), one_hot(slot == iota((ROWS, OWNERS * CAP), 1)))
    ids = sent[0:1] * 32.0 + sent[1:2] + sent[2:3] - 1.0
    for o in range(OWNERS):
        ids_ref[o : o + 1, :] = ids[:, o * CAP : (o + 1) * CAP].astype(jnp.int32)


def centres_kernel(ids_ref, centroids_ref, out_ref, pick_ref):
    @pl.when(pl.program_id(0) == 0)
    def _():
        ids = ids_ref[...].astype(F32).T.astype(jnp.int32)
        for s in range(OWNERS):
            at = slice(s * CAP, (s + 1) * CAP)
            pick_ref[at] = one_hot(ids[:, s : s + 1] == iota((CAP, LISTS), 1))

    out_ref[...] = dot(pick_ref[...], centroids_ref[...]).astype(BF16)


def codes_kernel(book_ref, stack_ref, turned_ref, norm_ref):
    for i in range(4):
        book = book_ref[i]
        high = book.astype(BF16)
        low = (book - high.astype(F32)).astype(BF16)
        stack_ref[i] = jnp.concatenate([high, low, high, low], axis=0)
        turned = jnp.concatenate([high.astype(F32), low.astype(F32)], axis=0).T
        turned_ref[i] = turned.astype(BF16)
        norm_ref[i] = INV_TEMP * jnp.sum(book * book, axis=0, keepdims=True)


def stats_kernel(
    tokens_ref, slot_ref, got_ref, rotation_ref, stack_ref, turned_ref, norm_ref,
    out_ref, res_ref, turned_res_ref,
):
    step = pl.program_id(0)

    @pl.when(step == 0)
    def _():
        pick = one_hot(slot_ref[...] == iota((ROWS, OWNERS * CAP), 1))
        centres = dot(pick, got_ref[...])
        res = (tokens_ref[...].astype(F32) - centres).astype(BF16)
        res_ref[...] = res
        turned_res_ref[...] = res.T

    rotated = dot(res_ref[...], rotation_ref[...])
    left = iota((ROWS, 2 * DSUB), 1) < DSUB
    pieces = []
    for pair in range(2):
        both = rotated[:, pair * 128 : (pair + 1) * 128]
        swapped = pltpu.roll(both, DSUB, 1)
        halves = []
        for side in range(2):
            m = 2 * pair + side
            twice = jnp.where(left, both, swapped) if side == 0 else jnp.where(left, swapped, both)
            high = twice.astype(BF16)
            rest = twice - high.astype(F32)
            low = rest.astype(BF16)
            logits = (2.0 * INV_TEMP) * dot(jnp.concatenate([high, low], axis=1), stack_ref[m]) - norm_ref[m]
            power = jnp.exp(logits - jnp.max(logits, axis=1, keepdims=True))
            prob = power * (1.0 / jnp.sum(power, axis=1, keepdims=True))
            mass = jnp.sum(prob, axis=0, keepdims=True)
            prob = prob.astype(BF16)
            split = jnp.where(left, high.astype(F32), rest).astype(BF16)
            num = dot(split, prob, 0, 0)
            at = pl.ds(pl.multiple_of(step * 256 + m * DSUB, DSUB), DSUB)
            out_ref[at, D : D + K] = (num[:DSUB] + num[DSUB:]).astype(BF16)
            row = iota((DSUB, 128), 0) % 32
            masses = jnp.where(row == 0, mass[:, :128], jnp.where(row == 1, mass[:, 128:], 0.0))
            out_ref[at, D + K :] = masses.astype(BF16)
            back = dot(prob, turned_ref[m])
            halves.append(back + pltpu.roll(back, DSUB, 1))
        pieces.append(jnp.where(left, halves[0], halves[1]).astype(BF16))
    cross = dot(turned_res_ref[...], jnp.concatenate(pieces, axis=1)).astype(BF16)
    for q in range(4):
        @pl.when(step == q)
        def _():
            for block in range(8):
                at = (block % 2) * 512 + (block // 2) * 128
                piece = cross[block * 128 : block * 128 + 128]
                out_ref[at : at + 128, q * 256 : (q + 1) * 256] = piece


def add_kernel(pair_ref, out_ref):
    total = (pair_ref[0].astype(F32) + pair_ref[1].astype(F32)).astype(BF16)
    w = iota((128, 128), 1)
    place = ((w >> 2) & 3) * 32 + (w >> 4) * 4 + (w & 3)
    out_ref[:, :D] = dot(one_hot(iota((128, 128), 0) == place), total[:, :D]).astype(BF16)
    out_ref[:, D:] = total[:, D:]


def pack_kernel(part_ref, out_ref):
    total = part_ref[0].astype(F32)
    for i in range(1, 16):
        total = total + part_ref[i].astype(F32)
    mass = jnp.concatenate([total[0:1, D + K :], total[1:2, D + K :], jnp.zeros((1, D - K), F32)], axis=1)
    high = mass.astype(BF16).astype(F32)
    mass = jnp.where(iota((4, D), 0) == 0, high, jnp.where(iota((4, D), 0) == 1, mass - high, 0.0))
    num = jnp.concatenate([total[8 * b : 8 * b + 8, D : D + K] for b in range(4)], axis=1)
    for z in range(8):
        head = jnp.concatenate([total[4 * z : 4 * z + 4, :D], mass], axis=0)
        out_ref[z] = jnp.concatenate([head, num], axis=0).astype(BF16)


def finish_kernel(part_ref, book_ref, cross_ref, fresh_ref):
    total = part_ref[0].astype(F32)
    for i in range(1, 8):
        total = total + part_ref[i].astype(F32)
    cross_ref[...] = total[0:4] * (1.0 / math.sqrt(ROWS * 256))
    count = total[4:5, :K] + total[5:6, :K] + 1.0
    for b in range(4):
        at = slice(8 * b, 8 * b + 8)
        fresh_ref[at] = (total[8:16, b * K : (b + 1) * K] + book_ref[at]) / count


def add(pair):
    return pl.pallas_call(
        add_kernel,
        grid=(4,),
        in_specs=[pl.BlockSpec((2, 128, WIDE), lambda i: (0, i, 0))],
        out_specs=pl.BlockSpec((128, WIDE), lambda i: (i, 0)),
        out_shape=jax.ShapeDtypeStruct((512, WIDE), BF16),
        name="add",
    )(pair)


def pack(part):
    return pl.pallas_call(
        pack_kernel, out_shape=jax.ShapeDtypeStruct((8, 16, D), BF16), name="pack"
    )(part)


def finish(part, book):
    return pl.pallas_call(
        finish_kernel,
        out_shape=(jax.ShapeDtypeStruct((4, D), F32), jax.ShapeDtypeStruct((32, K), F32)),
        name="finish",
    )(part, book)


def whole(shape):
    return pl.BlockSpec(shape, lambda *_: (0,) * len(shape))


def find_slots(owner, lists):
    return pl.pallas_call(
        slots_kernel,
        out_shape=(
            jax.ShapeDtypeStruct((ROWS, 1), jnp.int32),
            jax.ShapeDtypeStruct((OWNERS, CAP), jnp.int32),
        ),
        name="slots",
    )(owner.reshape(1, ROWS), lists.reshape(1, ROWS))


def find_centres(ids, centroids):
    columns = pl.BlockSpec((LISTS, 256), lambda i: (0, i))
    return pl.pallas_call(
        centres_kernel,
        grid=(D // 256,),
        in_specs=[whole((OWNERS, CAP)), columns],
        out_specs=columns,
        out_shape=jax.ShapeDtypeStruct((OWNERS * CAP, D), BF16),
        scratch_shapes=[pltpu.VMEM((OWNERS * CAP, LISTS), BF16)],
        name="centres",
    )(ids, centroids).reshape(OWNERS, CAP, D)


def split_codes(codebook):
    def block(*shape):
        return pl.BlockSpec((4, *shape), lambda i: (i, 0, 0))

    return pl.pallas_call(
        codes_kernel,
        grid=(M // 4,),
        in_specs=[block(DSUB, K)],
        out_specs=(block(4 * DSUB, K), block(K, 2 * DSUB), block(1, K)),
        out_shape=(
            jax.ShapeDtypeStruct((M, 4 * DSUB, K), BF16),
            jax.ShapeDtypeStruct((M, K, 2 * DSUB), BF16),
            jax.ShapeDtypeStruct((M, 1, K), F32),
        ),
        name="codes",
    )(codebook)


def code_stats(tokens, slot, got, rotation, codes):
    def block(*shape):
        return pl.BlockSpec((4, *shape), lambda i: (i, 0, 0))

    return pl.pallas_call(
        stats_kernel,
        grid=(M // 4,),
        in_specs=[
            whole((ROWS, D)),
            whole((ROWS, 1)),
            whole((OWNERS * CAP, D)),
            pl.BlockSpec((D, 256), lambda i: (0, i)),
            block(4 * DSUB, K),
            block(K, 2 * DSUB),
            block(1, K),
        ],
        out_specs=whole((D, WIDE)),
        out_shape=jax.ShapeDtypeStruct((D, WIDE), BF16),
        scratch_shapes=[pltpu.VMEM((ROWS, D), BF16), pltpu.VMEM((D, ROWS), BF16)],
        name="stats",
    )(tokens, slot, got, rotation, *codes)


def swap(value, axis):
    return lax.all_to_all(value, axis, split_axis=0, concat_axis=0, tiled=True)


def sent_to_all(value, axis):
    copies = jnp.broadcast_to(value, (lax.axis_size(axis), *value.shape))
    return swap(copies, axis).reshape(-1, value.shape[-1])


def local(tokens, owner, list_local, centroids, rotation, codebook):
    slot, ids = find_slots(owner, list_local)
    centres = find_centres(swap(ids, GRP), centroids)
    got = swap(centres, GRP).reshape(OWNERS * CAP, D)
    part = code_stats(tokens, slot, got, rotation, split_codes(codebook))
    part = add(swap(part.reshape(2, 512, WIDE), "c"))
    part = swap(pack(swap(part.reshape(16, 32, WIDE), XY)), "z")
    place = lax.axis_index("c") * 16 + lax.axis_index(XY)
    book = lax.dynamic_slice_in_dim(codebook.reshape(M * DSUB, K), place * 32, 32, 0)
    cross_cov, fresh = finish(part, book)
    fresh = sent_to_all(sent_to_all(fresh, XY), "c")
    return (fresh.reshape(M, DSUB, K), cross_cov)


def solution(mesh):
    finer = Mesh(mesh.devices.reshape(4, 2, 8, 4), ALL)
    in_specs = (P(ALL, None), P(ALL, None), P(ALL), P(ALL, None), P(), P())
    out_specs = (P(), P(ALL, None))
    return jax.shard_map(local, mesh=finer, in_specs=in_specs, out_specs=out_specs, check_vma=False)
```

```python
import math

import jax
import jax.numpy as jnp
from jax import lax
from jax.experimental import pallas as pl
from jax.experimental.pallas import tpu as pltpu
from jax.sharding import Mesh
from jax.sharding import PartitionSpec as P

ALL = ("x", "c", "z", "y")
GRP = ("x", "c")
XY = ("x", "y")
OWNERS = 8
CAP = 128
LISTS = 1024
ROWS = 512
D = 1024
M = 16
DSUB = 64
K = 256
WIDE = D + K + 128
INV_TEMP = 0.2
F32 = jnp.float32
BF16 = jnp.bfloat16


def dot(a, b, ca=1, cb=0):
    return lax.dot_general(a, b, (((ca,), (cb,)), ((), ())), preferred_element_type=F32)


def iota(shape, dim):
    return lax.broadcasted_iota(jnp.int32, shape, dim)


def one_hot(hit):
    return jnp.where(hit, 1.0, 0.0).astype(BF16)


def slots_kernel(owner_ref, lists_ref, slot_ref, ids_ref):
    owner = jnp.broadcast_to(owner_ref[...].astype(F32), (128, ROWS)).T[:, 0:1].astype(jnp.int32)
    mine = owner == iota((ROWS, 128), 1)
    earlier = one_hot(iota((ROWS, ROWS), 0) > iota((ROWS, ROWS), 1))
    before = dot(earlier, one_hot(mine))
    position = jnp.sum(jnp.where(mine, before, 0.0), axis=1, keepdims=True)
    slot = owner * CAP + position.astype(jnp.int32)
    slot_ref[...] = slot
    lists = lists_ref[...]
    row = iota((8, ROWS), 0)
    parts = jnp.where(row == 0, lists >> 5, jnp.where(row == 1, lists & 31, 1))
    sent = dot(parts.astype(F32).astype(BF16), one_hot(slot == iota((ROWS, OWNERS * CAP), 1)))
    ids = sent[0:1] * 32.0 + sent[1:2] + sent[2:3] - 1.0
    for o in range(OWNERS):
        ids_ref[o : o + 1, :] = ids[:, o * CAP : (o + 1) * CAP].astype(jnp.int32)


def centres_kernel(ids_ref, centroids_ref, out_ref, pick_ref):
    @pl.when(pl.program_id(0) == 0)
    def _():
        ids = ids_ref[...].astype(F32).T.astype(jnp.int32)
        for s in range(OWNERS):
            at = slice(s * CAP, (s + 1) * CAP)
            pick_ref[at] = one_hot(ids[:, s : s + 1] == iota((CAP, LISTS), 1))

    out_ref[...] = dot(pick_ref[...], centroids_ref[...]).astype(BF16)


def codes_kernel(book_ref, stack_ref, turned_ref, norm_ref):
    for i in range(4):
        book = book_ref[i]
        high = book.astype(BF16)
        low = (book - high.astype(F32)).astype(BF16)
        stack_ref[i] = jnp.concatenate([high, low, high, low], axis=0)
        turned = jnp.concatenate([high.astype(F32), low.astype(F32)], axis=0).T
        turned_ref[i] = turned.astype(BF16)
        norm_ref[i] = INV_TEMP * jnp.sum(book * book, axis=0, keepdims=True)


def stats_kernel(
    tokens_ref, slot_ref, got_ref, rotation_ref, stack_ref, turned_ref, norm_ref,
    out_ref, res_ref, turned_res_ref,
):
    step = pl.program_id(0)

    @pl.when(step == 0)
    def _():
        pick = one_hot(slot_ref[...] == iota((ROWS, OWNERS * CAP), 1))
        centres = dot(pick, got_ref[...])
        res = (tokens_ref[...].astype(F32) - centres).astype(BF16)
        res_ref[...] = res
        d = iota((D, D), 1)
        place = (
            ((d >> 7) & 1) * 512 + (d >> 8) * 128 + ((d >> 2) & 3) * 32 + ((d >> 4) & 7) * 4
        ) + (d & 3)
        turned_res_ref[...] = dot(one_hot(iota((D, D), 0) == place), res, 1, 1).astype(BF16)

    rotated = dot(res_ref[...], rotation_ref[...])
    left = iota((ROWS, 2 * DSUB), 1) < DSUB
    pieces = []
    for pair in range(2):
        both = rotated[:, pair * 128 : (pair + 1) * 128]
        swapped = pltpu.roll(both, DSUB, 1)
        halves = []
        for side in range(2):
            m = 2 * pair + side
            twice = jnp.where(left, both, swapped) if side == 0 else jnp.where(left, swapped, both)
            high = twice.astype(BF16)
            rest = twice - high.astype(F32)
            low = rest.astype(BF16)
            logits = (2.0 * INV_TEMP) * dot(jnp.concatenate([high, low], axis=1), stack_ref[m]) - norm_ref[m]
            power = jnp.exp(logits - jnp.max(logits, axis=1, keepdims=True))
            prob = power * (1.0 / jnp.sum(power, axis=1, keepdims=True))
            mass = jnp.sum(prob, axis=0, keepdims=True)
            prob = prob.astype(BF16)
            split = jnp.where(left, high.astype(F32), rest).astype(BF16)
            num = dot(split, prob, 0, 0)
            at = pl.ds(pl.multiple_of(step * 256 + m * DSUB, DSUB), DSUB)
            out_ref[at, D : D + K] = (num[:DSUB] + num[DSUB:]).astype(BF16)
            row = iota((DSUB, 128), 0) % 32
            masses = jnp.where(row == 0, mass[:, :128], jnp.where(row == 1, mass[:, 128:], 0.0))
            out_ref[at, D + K :] = masses.astype(BF16)
            back = dot(prob, turned_ref[m])
            halves.append(back + pltpu.roll(back, DSUB, 1))
        pieces.append(jnp.where(left, halves[0], halves[1]).astype(BF16))
    cross = dot(turned_res_ref[...], jnp.concatenate(pieces, axis=1)).astype(BF16)
    for q in range(4):
        @pl.when(step == q)
        def _():
            out_ref[:, q * 256 : (q + 1) * 256] = cross


def pack_kernel(part_ref, out_ref):
    total = part_ref[...]
    mass = jnp.concatenate([total[0:1, D + K :], total[1:2, D + K :], jnp.zeros((1, D - K), F32)], axis=1)
    high = mass.astype(BF16).astype(F32)
    mass = jnp.where(iota((4, D), 0) == 0, high, jnp.where(iota((4, D), 0) == 1, mass - high, 0.0))
    num = jnp.concatenate([total[8 * b : 8 * b + 8, D : D + K] for b in range(4)], axis=1)
    for z in range(8):
        head = jnp.concatenate([total[4 * z : 4 * z + 4, :D], mass], axis=0)
        out_ref[z] = jnp.concatenate([head, num], axis=0).astype(BF16)


def pack(part):
    return pl.pallas_call(
        pack_kernel, out_shape=jax.ShapeDtypeStruct((8, 16, D), BF16), name="pack"
    )(part)


def whole(shape):
    return pl.BlockSpec(shape, lambda *_: (0,) * len(shape))


def find_slots(owner, lists):
    return pl.pallas_call(
        slots_kernel,
        out_shape=(
            jax.ShapeDtypeStruct((ROWS, 1), jnp.int32),
            jax.ShapeDtypeStruct((OWNERS, CAP), jnp.int32),
        ),
        name="slots",
    )(owner.reshape(1, ROWS), lists.reshape(1, ROWS))


def find_centres(ids, centroids):
    columns = pl.BlockSpec((LISTS, 256), lambda i: (0, i))
    return pl.pallas_call(
        centres_kernel,
        grid=(D // 256,),
        in_specs=[whole((OWNERS, CAP)), columns],
        out_specs=columns,
        out_shape=jax.ShapeDtypeStruct((OWNERS * CAP, D), BF16),
        scratch_shapes=[pltpu.VMEM((OWNERS * CAP, LISTS), BF16)],
        name="centres",
    )(ids, centroids).reshape(OWNERS, CAP, D)


def split_codes(codebook):
    def block(*shape):
        return pl.BlockSpec((4, *shape), lambda i: (i, 0, 0))

    return pl.pallas_call(
        codes_kernel,
        grid=(M // 4,),
        in_specs=[block(DSUB, K)],
        out_specs=(block(4 * DSUB, K), block(K, 2 * DSUB), block(1, K)),
        out_shape=(
            jax.ShapeDtypeStruct((M, 4 * DSUB, K), BF16),
            jax.ShapeDtypeStruct((M, K, 2 * DSUB), BF16),
            jax.ShapeDtypeStruct((M, 1, K), F32),
        ),
        name="codes",
    )(codebook)


def code_stats(tokens, slot, got, rotation, codes):
    def block(*shape):
        return pl.BlockSpec((4, *shape), lambda i: (i, 0, 0))

    return pl.pallas_call(
        stats_kernel,
        grid=(M // 4,),
        in_specs=[
            whole((ROWS, D)),
            whole((ROWS, 1)),
            whole((OWNERS * CAP, D)),
            pl.BlockSpec((D, 256), lambda i: (0, i)),
            block(4 * DSUB, K),
            block(K, 2 * DSUB),
            block(1, K),
        ],
        out_specs=whole((D, WIDE)),
        out_shape=jax.ShapeDtypeStruct((D, WIDE), BF16),
        scratch_shapes=[pltpu.VMEM((ROWS, D), BF16), pltpu.VMEM((D, ROWS), BF16)],
        name="stats",
    )(tokens, slot, got, rotation, *codes)


def swap(value, axis):
    return lax.all_to_all(value, axis, split_axis=0, concat_axis=0, tiled=True)


def sent_to_all(value, axis):
    copies = jnp.broadcast_to(value, (lax.axis_size(axis), *value.shape))
    return swap(copies, axis).reshape(-1, value.shape[-1])


def local(tokens, owner, list_local, centroids, rotation, codebook):
    slot, ids = find_slots(owner, list_local)
    centres = find_centres(swap(ids, GRP), centroids)
    got = swap(centres, GRP).reshape(OWNERS * CAP, D)
    part = code_stats(tokens, slot, got, rotation, split_codes(codebook))
    part = swap(part.reshape(2, 512, WIDE), "c").astype(F32).sum(axis=0).astype(BF16)
    part = swap(part.reshape(16, 32, WIDE), XY).astype(F32).sum(axis=0)
    part = swap(pack(part), "z").astype(F32).sum(axis=0)
    cross_cov = part[:4] * (1.0 / math.sqrt(ROWS * 256))
    place = lax.axis_index("c") * 16 + lax.axis_index(XY)
    book = lax.dynamic_slice_in_dim(codebook.reshape(M * DSUB, K), place * 32, 32, 0)
    num = jnp.concatenate([part[8:, b * K : (b + 1) * K] for b in range(4)], axis=0)
    fresh = (num + book) / (part[4:5, :K] + part[5:6, :K] + 1.0)
    fresh = sent_to_all(sent_to_all(fresh, XY), "c")
    return (fresh.reshape(M, DSUB, K), cross_cov)


def solution(mesh):
    finer = Mesh(mesh.devices.reshape(4, 2, 8, 4), ALL)
    in_specs = (P(ALL, None), P(ALL, None), P(ALL), P(ALL, None), P(), P())
    out_specs = (P(), P(ALL, None))
    return jax.shard_map(local, mesh=finer, in_specs=in_specs, out_specs=out_specs, check_vma=False)
```

```python
import math

import jax
import jax.numpy as jnp
from jax import lax
from jax.experimental import pallas as pl
from jax.experimental.pallas import tpu as pltpu
from jax.sharding import Mesh
from jax.sharding import PartitionSpec as P

ALL = ("x", "c", "z", "y")
GRP = ("x", "c")
XY = ("x", "y")
OWNERS = 8
CAP = 128
LISTS = 1024
ROWS = 512
D = 1024
M = 16
DSUB = 64
K = 256
WIDE = D + K + 128
INV_TEMP = 0.2
F32 = jnp.float32
BF16 = jnp.bfloat16


def dot(a, b, ca=1, cb=0):
    return lax.dot_general(a, b, (((ca,), (cb,)), ((), ())), preferred_element_type=F32)


def iota(shape, dim):
    return lax.broadcasted_iota(jnp.int32, shape, dim)


def one_hot(hit):
    return jnp.where(hit, 1.0, 0.0).astype(BF16)


def slots_kernel(owner_ref, lists_ref, slot_ref, ids_ref):
    owner = jnp.broadcast_to(owner_ref[...].astype(F32), (128, ROWS)).T[:, 0:1].astype(jnp.int32)
    mine = owner == iota((ROWS, 128), 1)
    earlier = one_hot(iota((ROWS, ROWS), 0) > iota((ROWS, ROWS), 1))
    before = dot(earlier, one_hot(mine))
    position = jnp.sum(jnp.where(mine, before, 0.0), axis=1, keepdims=True)
    slot = owner * CAP + position.astype(jnp.int32)
    slot_ref[...] = slot
    lists = lists_ref[...]
    row = iota((8, ROWS), 0)
    parts = jnp.where(row == 0, lists >> 5, jnp.where(row == 1, lists & 31, 1))
    sent = dot(parts.astype(F32).astype(BF16), one_hot(slot == iota((ROWS, OWNERS * CAP), 1)))
    ids = sent[0:1] * 32.0 + sent[1:2] + sent[2:3] - 1.0
    for o in range(OWNERS):
        ids_ref[o : o + 1, :] = ids[:, o * CAP : (o + 1) * CAP].astype(jnp.int32)


def centres_kernel(ids_ref, centroids_ref, out_ref, pick_ref):
    @pl.when(pl.program_id(0) == 0)
    def _():
        ids = ids_ref[...].astype(F32).T.astype(jnp.int32)
        for s in range(OWNERS):
            at = slice(s * CAP, (s + 1) * CAP)
            pick_ref[at] = one_hot(ids[:, s : s + 1] == iota((CAP, LISTS), 1))

    out_ref[...] = dot(pick_ref[...], centroids_ref[...]).astype(BF16)


def codes_kernel(book_ref, stack_ref, turned_ref, norm_ref):
    for i in range(4):
        book = book_ref[i]
        high = book.astype(BF16)
        low = (book - high.astype(F32)).astype(BF16)
        stack_ref[i] = jnp.concatenate([high, low, high, low], axis=0)
        turned = jnp.concatenate([high.astype(F32), low.astype(F32)], axis=0).T
        turned_ref[i] = turned.astype(BF16)
        norm_ref[i] = INV_TEMP * jnp.sum(book * book, axis=0, keepdims=True)


def stats_kernel(
    tokens_ref, slot_ref, got_ref, rotation_ref, stack_ref, turned_ref, norm_ref,
    out_ref, res_ref, turned_res_ref,
):
    step = pl.program_id(0)

    @pl.when(step == 0)
    def _():
        pick = one_hot(slot_ref[...] == iota((ROWS, OWNERS * CAP), 1))
        centres = dot(pick, got_ref[...])
        res = (tokens_ref[...].astype(F32) - centres).astype(BF16)
        res_ref[...] = res
        d = iota((D, D), 1)
        place = (
            ((d >> 7) & 1) * 512 + (d >> 8) * 128 + ((d >> 2) & 3) * 32 + ((d >> 4) & 7) * 4
        ) + (d & 3)
        turned_res_ref[...] = dot(one_hot(iota((D, D), 0) == place), res, 1, 1).astype(BF16)

    rotated = dot(res_ref[...], rotation_ref[...])
    left = iota((ROWS, 2 * DSUB), 1) < DSUB
    pieces = []
    for pair in range(2):
        both = rotated[:, pair * 128 : (pair + 1) * 128]
        swapped = pltpu.roll(both, DSUB, 1)
        halves = []
        for side in range(2):
            m = 2 * pair + side
            twice = jnp.where(left, both, swapped) if side == 0 else jnp.where(left, swapped, both)
            high = twice.astype(BF16)
            rest = twice - high.astype(F32)
            low = rest.astype(BF16)
            logits = (2.0 * INV_TEMP) * dot(jnp.concatenate([high, low], axis=1), stack_ref[m]) - norm_ref[m]
            power = jnp.exp(logits - jnp.max(logits, axis=1, keepdims=True))
            prob = power * (1.0 / jnp.sum(power, axis=1, keepdims=True))
            mass = jnp.sum(prob, axis=0, keepdims=True)
            prob = prob.astype(BF16)
            split = jnp.where(left, high.astype(F32), rest).astype(BF16)
            num = dot(split, prob, 0, 0)
            at = pl.ds(pl.multiple_of(step * 256 + m * DSUB, DSUB), DSUB)
            out_ref[at, D : D + K] = (num[:DSUB] + num[DSUB:]).astype(BF16)
            row = iota((DSUB, 128), 0) % 32
            masses = jnp.where(row == 0, mass[:, :128], jnp.where(row == 1, mass[:, 128:], 0.0))
            out_ref[at, D + K :] = masses.astype(BF16)
            back = dot(prob, turned_ref[m])
            halves.append(back + pltpu.roll(back, DSUB, 1))
        pieces.append(jnp.where(left, halves[0], halves[1]).astype(BF16))
    cross = dot(turned_res_ref[...], jnp.concatenate(pieces, axis=1)).astype(BF16)
    for q in range(4):
        @pl.when(step == q)
        def _():
            out_ref[:, q * 256 : (q + 1) * 256] = cross


def pack_kernel(part_ref, out_ref):
    total = part_ref[...]
    mass = jnp.concatenate([total[0:1, D + K :], total[1:2, D + K :], jnp.zeros((1, D - K), F32)], axis=1)
    high = mass.astype(BF16).astype(F32)
    mass = jnp.where(iota((4, D), 0) == 0, high, jnp.where(iota((4, D), 0) == 1, mass - high, 0.0))
    num = jnp.concatenate([total[8 * b : 8 * b + 8, D : D + K] for b in range(4)], axis=1)
    for z in range(8):
        head = jnp.concatenate([total[4 * z : 4 * z + 4, :D], mass], axis=0)
        out_ref[z] = jnp.concatenate([head, num], axis=0).astype(BF16)


def pack(part):
    return pl.pallas_call(
        pack_kernel, out_shape=jax.ShapeDtypeStruct((8, 16, D), BF16), name="pack"
    )(part)


def whole(shape):
    return pl.BlockSpec(shape, lambda *_: (0,) * len(shape))


def find_slots(owner, lists):
    return pl.pallas_call(
        slots_kernel,
        out_shape=(
            jax.ShapeDtypeStruct((ROWS, 1), jnp.int32),
            jax.ShapeDtypeStruct((OWNERS, CAP), jnp.int32),
        ),
        name="slots",
    )(owner.reshape(1, ROWS), lists.reshape(1, ROWS))


def find_centres(ids, centroids):
    columns = pl.BlockSpec((LISTS, 256), lambda i: (0, i))
    return pl.pallas_call(
        centres_kernel,
        grid=(D // 256,),
        in_specs=[whole((OWNERS, CAP)), columns],
        out_specs=columns,
        out_shape=jax.ShapeDtypeStruct((OWNERS * CAP, D), BF16),
        scratch_shapes=[pltpu.VMEM((OWNERS * CAP, LISTS), BF16)],
        name="centres",
    )(ids, centroids).reshape(OWNERS, CAP, D)


def split_codes(codebook):
    def block(*shape):
        return pl.BlockSpec((4, *shape), lambda i: (i, 0, 0))

    return pl.pallas_call(
        codes_kernel,
        grid=(M // 4,),
        in_specs=[block(DSUB, K)],
        out_specs=(block(4 * DSUB, K), block(K, 2 * DSUB), block(1, K)),
        out_shape=(
            jax.ShapeDtypeStruct((M, 4 * DSUB, K), BF16),
            jax.ShapeDtypeStruct((M, K, 2 * DSUB), BF16),
            jax.ShapeDtypeStruct((M, 1, K), F32),
        ),
        name="codes",
    )(codebook)


def code_stats(tokens, slot, got, rotation, codes):
    def block(*shape):
        return pl.BlockSpec((4, *shape), lambda i: (i, 0, 0))

    return pl.pallas_call(
        stats_kernel,
        grid=(M // 4,),
        in_specs=[
            whole((ROWS, D)),
            whole((ROWS, 1)),
            whole((OWNERS * CAP, D)),
            pl.BlockSpec((D, 256), lambda i: (0, i)),
            block(4 * DSUB, K),
            block(K, 2 * DSUB),
            block(1, K),
        ],
        out_specs=whole((D, WIDE)),
        out_shape=jax.ShapeDtypeStruct((D, WIDE), BF16),
        scratch_shapes=[pltpu.VMEM((ROWS, D), BF16), pltpu.VMEM((D, ROWS), BF16)],
        name="stats",
    )(tokens, slot, got, rotation, *codes)


def swap(value, axis):
    return lax.all_to_all(value, axis, split_axis=0, concat_axis=0, tiled=True)


def with_pair(value):
    return lax.ppermute(value, "c", [(0, 1), (1, 0)])


def sent_to_all(value, axis):
    copies = jnp.broadcast_to(value, (lax.axis_size(axis), *value.shape))
    return swap(copies, axis).reshape(-1, value.shape[-1])


def local(tokens, owner, list_local, centroids, rotation, codebook):
    slot, ids = find_slots(owner, list_local)
    centres = find_centres(swap(ids, GRP), centroids)
    got = swap(centres, GRP).reshape(OWNERS * CAP, D)
    part = code_stats(tokens, slot, got, rotation, split_codes(codebook))
    core = lax.axis_index("c")
    halves = part.reshape(2, 512, WIDE)
    mine = lax.dynamic_index_in_dim(halves, core, 0, keepdims=False)
    other = lax.dynamic_index_in_dim(halves, 1 - core, 0, keepdims=False)
    part = (mine.astype(F32) + with_pair(other).astype(F32)).astype(BF16)
    part = swap(part.reshape(16, 32, WIDE), XY).astype(F32).sum(axis=0)
    part = swap(pack(part), "z").astype(F32).sum(axis=0)
    cross_cov = part[:4] * (1.0 / math.sqrt(ROWS * 256))
    place = lax.axis_index("c") * 16 + lax.axis_index(XY)
    book = lax.dynamic_slice_in_dim(codebook.reshape(M * DSUB, K), place * 32, 32, 0)
    num = jnp.concatenate([part[8:, b * K : (b + 1) * K] for b in range(4)], axis=0)
    fresh = (num + book) / (part[4:5, :K] + part[5:6, :K] + 1.0)
    fresh = sent_to_all(fresh, XY)
    other = with_pair(fresh)
    fresh = jnp.where(core == 0, jnp.stack([fresh, other]), jnp.stack([other, fresh]))
    return (fresh.reshape(M, DSUB, K), cross_cov)


def solution(mesh):
    finer = Mesh(mesh.devices.reshape(4, 2, 8, 4), ALL)
    in_specs = (P(ALL, None), P(ALL, None), P(ALL), P(ALL, None), P(), P())
    out_specs = (P(), P(ALL, None))
    return jax.shard_map(local, mesh=finer, in_specs=in_specs, out_specs=out_specs, check_vma=False)
```

```python
import math

import jax
import jax.numpy as jnp
from jax import lax
from jax.experimental import pallas as pl
from jax.experimental.pallas import tpu as pltpu
from jax.sharding import Mesh
from jax.sharding import PartitionSpec as P

ALL = ("x", "c", "z", "y")
GRP = ("x", "c")
XY = ("x", "y")
OWNERS = 8
CAP = 128
LISTS = 1024
ROWS = 512
D = 1024
M = 16
DSUB = 64
K = 256
WIDE = D + K + 128
INV_TEMP = 0.2
F32 = jnp.float32
BF16 = jnp.bfloat16


def dot(a, b, ca=1, cb=0):
    return lax.dot_general(a, b, (((ca,), (cb,)), ((), ())), preferred_element_type=F32)


def iota(shape, dim):
    return lax.broadcasted_iota(jnp.int32, shape, dim)


def one_hot(hit):
    return jnp.where(hit, 1.0, 0.0).astype(BF16)


def slots_kernel(owner_ref, lists_ref, slot_ref, ids_ref):
    owner = jnp.broadcast_to(owner_ref[...].astype(F32), (128, ROWS)).T[:, 0:1].astype(jnp.int32)
    mine = owner == iota((ROWS, 128), 1)
    earlier = one_hot(iota((ROWS, ROWS), 0) > iota((ROWS, ROWS), 1))
    before = dot(earlier, one_hot(mine))
    position = jnp.sum(jnp.where(mine, before, 0.0), axis=1, keepdims=True)
    slot = owner * CAP + position.astype(jnp.int32)
    slot_ref[...] = slot
    lists = lists_ref[...]
    row = iota((8, ROWS), 0)
    parts = jnp.where(row == 0, lists >> 5, jnp.where(row == 1, lists & 31, 1))
    sent = dot(parts.astype(F32).astype(BF16), one_hot(slot == iota((ROWS, OWNERS * CAP), 1)))
    ids = sent[0:1] * 32.0 + sent[1:2] + sent[2:3] - 1.0
    for o in range(OWNERS):
        ids_ref[o : o + 1, :] = ids[:, o * CAP : (o + 1) * CAP].astype(jnp.int32)


def centres_kernel(ids_ref, centroids_ref, out_ref, pick_ref):
    @pl.when(pl.program_id(0) == 0)
    def _():
        ids = ids_ref[...].astype(F32).T.astype(jnp.int32)
        for s in range(OWNERS):
            at = slice(s * CAP, (s + 1) * CAP)
            pick_ref[at] = one_hot(ids[:, s : s + 1] == iota((CAP, LISTS), 1))

    out_ref[...] = dot(pick_ref[...], centroids_ref[...]).astype(BF16)


def codes_kernel(book_ref, stack_ref, turned_ref, norm_ref):
    for i in range(4):
        book = book_ref[i]
        high = book.astype(BF16)
        low = (book - high.astype(F32)).astype(BF16)
        stack_ref[i] = jnp.concatenate([high, low, high, low], axis=0)
        turned = jnp.concatenate([high.astype(F32), low.astype(F32)], axis=0).T
        turned_ref[i] = turned.astype(BF16)
        norm_ref[i] = INV_TEMP * jnp.sum(book * book, axis=0, keepdims=True)


def stats_kernel(
    core_ref, tokens_ref, slot_ref, got_ref, rotation_ref, stack_ref, turned_ref, norm_ref,
    out_ref, res_ref, turned_res_ref,
):
    step = pl.program_id(0)

    @pl.when(step == 0)
    def _():
        pick = one_hot(slot_ref[...] == iota((ROWS, OWNERS * CAP), 1))
        centres = dot(pick, got_ref[...])
        res = (tokens_ref[...].astype(F32) - centres).astype(BF16)
        res_ref[...] = res
        d = iota((D, D), 1)
        place = (
            (((d >> 7) & 1) ^ core_ref[0]) * 512 + (d >> 8) * 128 + ((d >> 2) & 3) * 32 + ((d >> 4) & 7) * 4
        ) + (d & 3)
        turned_res_ref[...] = dot(one_hot(iota((D, D), 0) == place), res, 1, 1).astype(BF16)

    rotated = dot(res_ref[...], rotation_ref[...])
    left = iota((ROWS, 2 * DSUB), 1) < DSUB
    pieces = []
    for pair in range(2):
        both = rotated[:, pair * 128 : (pair + 1) * 128]
        swapped = pltpu.roll(both, DSUB, 1)
        halves = []
        for side in range(2):
            m = 2 * pair + side
            twice = jnp.where(left, both, swapped) if side == 0 else jnp.where(left, swapped, both)
            high = twice.astype(BF16)
            rest = twice - high.astype(F32)
            low = rest.astype(BF16)
            logits = (2.0 * INV_TEMP) * dot(jnp.concatenate([high, low], axis=1), stack_ref[m]) - norm_ref[m]
            power = jnp.exp(logits - jnp.max(logits, axis=1, keepdims=True))
            prob = power * (1.0 / jnp.sum(power, axis=1, keepdims=True))
            mass = jnp.sum(prob, axis=0, keepdims=True)
            prob = prob.astype(BF16)
            split = jnp.where(left, high.astype(F32), rest).astype(BF16)
            num = dot(split, prob, 0, 0)
            at = pl.ds(pl.multiple_of((step * 256 + m * DSUB + core_ref[0] * 512) & (D - 1), DSUB), DSUB)
            out_ref[at, D : D + K] = (num[:DSUB] + num[DSUB:]).astype(BF16)
            row = iota((DSUB, 128), 0) % 32
            masses = jnp.where(row == 0, mass[:, :128], jnp.where(row == 1, mass[:, 128:], 0.0))
            out_ref[at, D + K :] = masses.astype(BF16)
            back = dot(prob, turned_ref[m])
            halves.append(back + pltpu.roll(back, DSUB, 1))
        pieces.append(jnp.where(left, halves[0], halves[1]).astype(BF16))
    cross = dot(turned_res_ref[...], jnp.concatenate(pieces, axis=1)).astype(BF16)
    for q in range(4):
        @pl.when(step == q)
        def _():
            out_ref[:, q * 256 : (q + 1) * 256] = cross


def pack_kernel(part_ref, out_ref):
    total = part_ref[...]
    mass = jnp.concatenate([total[0:1, D + K :], total[1:2, D + K :], jnp.zeros((1, D - K), F32)], axis=1)
    high = mass.astype(BF16).astype(F32)
    mass = jnp.where(iota((4, D), 0) == 0, high, jnp.where(iota((4, D), 0) == 1, mass - high, 0.0))
    num = jnp.concatenate([total[8 * b : 8 * b + 8, D : D + K] for b in range(4)], axis=1)
    for z in range(8):
        head = jnp.concatenate([total[4 * z : 4 * z + 4, :D], mass], axis=0)
        out_ref[z] = jnp.concatenate([head, num], axis=0).astype(BF16)


def pack(part):
    return pl.pallas_call(
        pack_kernel, out_shape=jax.ShapeDtypeStruct((8, 16, D), BF16), name="pack"
    )(part)


def whole(shape):
    return pl.BlockSpec(shape, lambda *_: (0,) * len(shape))


def find_slots(owner, lists):
    return pl.pallas_call(
        slots_kernel,
        out_shape=(
            jax.ShapeDtypeStruct((ROWS, 1), jnp.int32),
            jax.ShapeDtypeStruct((OWNERS, CAP), jnp.int32),
        ),
        name="slots",
    )(owner.reshape(1, ROWS), lists.reshape(1, ROWS))


def find_centres(ids, centroids):
    columns = pl.BlockSpec((LISTS, 256), lambda i: (0, i))
    return pl.pallas_call(
        centres_kernel,
        grid=(D // 256,),
        in_specs=[whole((OWNERS, CAP)), columns],
        out_specs=columns,
        out_shape=jax.ShapeDtypeStruct((OWNERS * CAP, D), BF16),
        scratch_shapes=[pltpu.VMEM((OWNERS * CAP, LISTS), BF16)],
        name="centres",
    )(ids, centroids).reshape(OWNERS, CAP, D)


def split_codes(codebook):
    def block(*shape):
        return pl.BlockSpec((4, *shape), lambda i: (i, 0, 0))

    return pl.pallas_call(
        codes_kernel,
        grid=(M // 4,),
        in_specs=[block(DSUB, K)],
        out_specs=(block(4 * DSUB, K), block(K, 2 * DSUB), block(1, K)),
        out_shape=(
            jax.ShapeDtypeStruct((M, 4 * DSUB, K), BF16),
            jax.ShapeDtypeStruct((M, K, 2 * DSUB), BF16),
            jax.ShapeDtypeStruct((M, 1, K), F32),
        ),
        name="codes",
    )(codebook)


def code_stats(core, tokens, slot, got, rotation, codes):
    def block(*shape):
        return pl.BlockSpec((4, *shape), lambda i: (i, 0, 0))

    return pl.pallas_call(
        stats_kernel,
        grid=(M // 4,),
        in_specs=[
            pl.BlockSpec(memory_space=pltpu.SMEM),
            whole((ROWS, D)),
            whole((ROWS, 1)),
            whole((OWNERS * CAP, D)),
            pl.BlockSpec((D, 256), lambda i: (0, i)),
            block(4 * DSUB, K),
            block(K, 2 * DSUB),
            block(1, K),
        ],
        out_specs=whole((D, WIDE)),
        out_shape=jax.ShapeDtypeStruct((D, WIDE), BF16),
        scratch_shapes=[pltpu.VMEM((ROWS, D), BF16), pltpu.VMEM((D, ROWS), BF16)],
        name="stats",
    )(core.reshape(1), tokens, slot, got, rotation, *codes)


def swap(value, axis):
    return lax.all_to_all(value, axis, split_axis=0, concat_axis=0, tiled=True)


def with_pair(value):
    return lax.ppermute(value, "c", [(0, 1), (1, 0)])


def sent_to_all(value, axis):
    copies = jnp.broadcast_to(value, (lax.axis_size(axis), *value.shape))
    return swap(copies, axis).reshape(-1, value.shape[-1])


def local(tokens, owner, list_local, centroids, rotation, codebook):
    slot, ids = find_slots(owner, list_local)
    centres = find_centres(swap(ids, GRP), centroids)
    got = swap(centres, GRP).reshape(OWNERS * CAP, D)
    core = lax.axis_index("c")
    part = code_stats(core, tokens, slot, got, rotation, split_codes(codebook))
    mine, other = part[:512], part[512:]
    part = (mine.astype(F32) + with_pair(other).astype(F32)).astype(BF16)
    part = swap(part.reshape(16, 32, WIDE), XY).astype(F32).sum(axis=0)
    part = swap(pack(part), "z").astype(F32).sum(axis=0)
    cross_cov = part[:4] * (1.0 / math.sqrt(ROWS * 256))
    place = lax.axis_index("c") * 16 + lax.axis_index(XY)
    book = lax.dynamic_slice_in_dim(codebook.reshape(M * DSUB, K), place * 32, 32, 0)
    num = jnp.concatenate([part[8:, b * K : (b + 1) * K] for b in range(4)], axis=0)
    fresh = (num + book) / (part[4:5, :K] + part[5:6, :K] + 1.0)
    fresh = sent_to_all(fresh, XY)
    other = with_pair(fresh)
    fresh = jnp.where(core == 0, jnp.stack([fresh, other]), jnp.stack([other, fresh]))
    return (fresh.reshape(M, DSUB, K), cross_cov)


def solution(mesh):
    finer = Mesh(mesh.devices.reshape(4, 2, 8, 4), ALL)
    in_specs = (P(ALL, None), P(ALL, None), P(ALL), P(ALL, None), P(), P())
    out_specs = (P(), P(ALL, None))
    return jax.shard_map(local, mesh=finer, in_specs=in_specs, out_specs=out_specs, check_vma=False)
```
